32 devices in a mesh: grp: 1, seq: 32 (over z, y, x, core).
Axes of the slice: x: 2, y: 2, z: 4, core: 2. Of those that a mesh axis runs over, the one named last changes fastest.
Arguments:
- features: bfloat16 [8192, 768], P(('grp', 'seq')), may hold values from -6 to 6
- targets: int32 [8192, 896], P(('grp', 'seq')), may hold values from 0 to 3
- mappable: int32 [8192], P(('grp', 'seq')), may hold values 0 or 1
- w_in: bfloat16 [2, 768, 384], replicated, may hold values from -0.21875 to 0.21875
- w_conv: bfloat16 [2, 3, 384, 384], replicated, may hold values from -0.1875 to 0.1875
- w_out: bfloat16 [2, 384, 768], replicated, may hold values from -0.3125 to 0.3125
- w_head: bfloat16 [768, 896], replicated, may hold values from -0.109375 to 0.109375
Outputs:
- grad_in: float32 [2, 768, 384], P('grp', 'seq')
- grad_conv: float32 [2, 3, 384, 384], P('grp', None, 'seq')
- grad_out: float32 [2, 384, 768], P('grp', 'seq')
The draws below stay inside these ranges and needn't reach their ends.
All inputs are finite; a program needn't handle non-finite values. No bound on the sum of `mappable` on one device may be relied on, other than what follows from the above.
Results may differ from the reference program's by a relative error of at most 0.0075.
Values may be sent and summed in bfloat16 or wider, within the bound.
A program may use at most 128 MiB of HBM per device.

```python
import math
import jax
import jax.numpy as jnp

D = 768
B = 384
TRACKS = 896
FIRST_DILATION = 2048
SECOND_DILATION = 4096
LEN = 8192


def set_ends(result, rng, least, largest):
    shape = result.shape
    index_at = [jax.random.randint(jax.random.fold_in(rng, axis), (), 0, shape[axis]) for axis in range(len(shape))]
    result = result.at[tuple(index_at)].set(least)
    longest = shape.index(max(shape))
    index_at[longest] = (index_at[longest] + 1) % shape[longest]
    return result.at[tuple(index_at)].set(largest)


def strengthened(drawn, own_key, source, target, parts, factor):
    owner, partner = [(jnp.arange(drawn.shape[dim]) // (drawn.shape[dim] // parts)).reshape([-1 if axis == dim else 1 for axis in range(drawn.ndim)]) for dim in (source, target)]
    chosen = jax.random.permutation(own_key, parts)[partner]
    strong = (owner == chosen) | (owner == (partner + parts // 2) % parts)
    return jnp.where(strong, factor * drawn, drawn)


def steps_of(own_key, extent, shards, low, top_value):
    loudness = 1.0
    for dim, shards_of in shards:
        heights = jax.random.uniform(jax.random.fold_in(jax.random.fold_in(own_key, 6), dim), (shards_of,), jnp.float32, low / len(shards), top_value / len(shards))
        loudness = loudness * jnp.repeat(jnp.exp(heights), extent[dim] // shards_of).reshape((-1,) + (1,) * (len(extent) - 1 - dim))
    return loudness


def normal_values(key, shape, scale, reach, pieces=(), kind=jnp.bfloat16):
    values = scale * jax.random.normal(key, shape, jnp.float32)
    if pieces:
        values = values * steps_of(key, shape, pieces, -0.22, 0.18)
    return jnp.clip(values, -reach, reach).astype(kind)


def noise_with(rng, extent, deviation, bound, split, heavy, kind=jnp.bfloat16):
    entries = deviation * jax.random.normal(rng, extent, jnp.float32)
    if split:
        entries = entries * steps_of(rng, extent, split, -0.22, 0.18)
    return jnp.clip(strengthened(entries, jax.random.fold_in(rng, 3), *heavy), -bound, bound).astype(kind)


def setup_inputs(seed: int = 0, part: int = 0) -> dict:
    key_of = jax.random.split(jax.random.key(seed), 8)
    part_keys = jax.random.split(jax.random.fold_in(key_of[7], part), 8)
    return {
        "features": noise_with(part_keys[0], (LEN, D), 1.0, 6.0, ((0, 32),), (0, 1, 32, 2.75)),
        "targets": set_ends(jax.random.randint(part_keys[1], (LEN, TRACKS), 0, 4), jax.random.fold_in(part_keys[1], 1), 0, 3).astype(jnp.int32),
        "mappable": set_ends((jax.random.randint(part_keys[2], (LEN,), 0, 8) < 7).astype(jnp.int32), jax.random.fold_in(part_keys[2], 1), 0, 1),
        "w_in": normal_values(key_of[3], (2, D, B), D ** -0.5, 0.21875),
        "w_conv": normal_values(key_of[4], (2, 3, B, B), (3 * B) ** -0.5, 0.1875),
        "w_out": normal_values(key_of[5], (2, B, D), B ** -0.5, 0.3125),
        "w_head": normal_values(key_of[6], (D, TRACKS), (4 * D) ** -0.5, 0.109375),
    }


TANH_COEF = 0.7978845608028654
CUBIC_COEF = 0.044715

def gelu_value(values):
    return jax.nn.gelu(values, approximate=True)

def gelu_slope(values):
    inner = TANH_COEF * (values + CUBIC_COEF * values * values * values)
    tangent = jnp.tanh(inner)
    return 0.5 * (1.0 + tangent) + 0.5 * values * (1.0 - tangent * tangent) * TANH_COEF * (1.0 + 3.0 * CUBIC_COEF * values * values)

def matmul(left, right):
    return jnp.dot(left, right, preferred_element_type=jnp.float32)

def strand_turn(array):
    return jnp.roll(array[::-1], array.shape[1] // 2, axis=1)

def received_earlier(array, shift_amount):
    filler = jnp.zeros((shift_amount, array.shape[1]), array.dtype)
    return jnp.concatenate([filler, array[:-shift_amount]], axis=0)

def from_after(array, shift_amount):
    filler = jnp.zeros((shift_amount, array.shape[1]), array.dtype)
    return jnp.concatenate([array[shift_amount:], filler], axis=0)

def reference(features, targets, mappable, w_in, w_conv, w_out, w_head):
    dilation_list = (FIRST_DILATION, SECOND_DILATION)
    finals = []
    records = []
    for strand in range(2):
        stream = features if strand == 0 else strand_turn(features)
        saved = []
        for layer in range(2):
            shift_amount = dilation_list[layer]
            before_gelu = matmul(stream, w_in[layer])
            hidden = gelu_value(before_gelu).astype(jnp.bfloat16)
            conv_sum = matmul(received_earlier(hidden, shift_amount), w_conv[layer, 0]) + matmul(hidden, w_conv[layer, 1]) + matmul(from_after(hidden, shift_amount), w_conv[layer, 2])
            middle = gelu_value(conv_sum).astype(jnp.bfloat16)
            saved.append((stream, before_gelu, hidden, conv_sum, middle))
            stream = (stream.astype(jnp.float32) + matmul(middle, w_out[layer])).astype(jnp.bfloat16)
        records.append(saved)
        finals.append(stream)
    joined = (0.5 * (finals[0].astype(jnp.float32) + strand_turn(finals[1]).astype(jnp.float32))).astype(jnp.bfloat16)
    logits = matmul(joined, w_head)
    loss_scale = 1.0 / math.sqrt(LEN)
    row_weight = mappable.astype(jnp.float32)[:, None]
    logit_grad = (row_weight * (jnp.exp(logits) - targets.astype(jnp.float32)) * loss_scale).astype(jnp.bfloat16)
    incoming = (0.5 * matmul(logit_grad, w_head.T)).astype(jnp.bfloat16)
    grads_in = [jnp.zeros((D, B), jnp.float32) for layer in range(2)]
    grads_out = [jnp.zeros((B, D), jnp.float32) for layer in range(2)]
    grads_tap = [[jnp.zeros((B, B), jnp.float32) for tap in range(3)] for layer in range(2)]
    for strand in range(2):
        cotangent = incoming if strand == 0 else strand_turn(incoming)
        for layer in (1, 0):
            stream, before_gelu, hidden, conv_sum, middle = records[strand][layer]
            shift_amount = dilation_list[layer]
            grads_out[layer] = grads_out[layer] + matmul(middle.T, cotangent)
            slope_mid = (matmul(cotangent, w_out[layer].T) * gelu_slope(conv_sum)).astype(jnp.bfloat16)
            later = from_after(slope_mid, shift_amount)
            earlier = received_earlier(slope_mid, shift_amount)
            grads_tap[layer][0] = grads_tap[layer][0] + matmul(hidden.T, later)
            grads_tap[layer][1] = grads_tap[layer][1] + matmul(hidden.T, slope_mid)
            grads_tap[layer][2] = grads_tap[layer][2] + matmul(hidden.T, earlier)
            hidden_backward = matmul(later, w_conv[layer, 0].T) + matmul(slope_mid, w_conv[layer, 1].T) + matmul(earlier, w_conv[layer, 2].T)
            slope_in = (hidden_backward * gelu_slope(before_gelu)).astype(jnp.bfloat16)
            grads_in[layer] = grads_in[layer] + matmul(stream.T, slope_in)
            if layer == 1:
                cotangent = (cotangent.astype(jnp.float32) + matmul(slope_in, w_in[layer].T)).astype(jnp.bfloat16)
    grad_in = jnp.stack(grads_in)
    grad_conv = jnp.stack([jnp.stack(grads_tap[layer]) for layer in range(2)])
    grad_out = jnp.stack(grads_out)
    return (grad_in, grad_conv, grad_out)
```

```python
import functools
import math

import jax
import jax.numpy as jnp
from jax import lax
from jax.experimental import pallas as pl
from jax.experimental.pallas import tpu as pltpu
from jax.sharding import PartitionSpec as P

FIRST_DILATION = 2048
SECOND_DILATION = 4096

TANH_COEF = 0.7978845608028654
CUBIC_COEF = 0.044715
LANES = 128
CHUNK = 32
BF16 = jnp.bfloat16
F32 = jnp.float32


def dot(left, right):
    return jnp.dot(left, right, preferred_element_type=F32)


def dot_t(left, right):
    return lax.dot_general(left, right, (((1,), (1,)), ((), ())), preferred_element_type=F32)


def grad_dot(left, right):
    return lax.dot_general(left, right, (((0,), (0,)), ((), ())), preferred_element_type=F32)


def kernel(
    n,
    features,
    packed,
    w_in_hbm,
    w_conv_hbm,
    w_out_hbm,
    w_head_hbm,
    out_in,
    out_conv,
    out_out,
    w_in,
    w_conv,
    w_out,
    w_head,
    stream,
    tracks_in,
    hidden,
    slope_h,
    middle,
    slope_m,
    cot,
    grad_v,
    narrow,
    wide,
    joined,
    logit_grad,
    sums,
    send0,
    recv0,
    send1,
    recv1,
    send2,
    recv2,
    send3,
    recv3,
    final,
    weight_sem,
    a_send,
    a_recv,
    g_send,
    g_recv,
):
    rows, channels = features.shape
    hid = w_in.shape[2]
    tracks = w_head.shape[1]
    links = rows * n // FIRST_DILATION
    part = rows // links
    stride = n // links
    me = lax.axis_index("seq")
    high = me // stride
    low = me % stride
    core = low % 2
    bit_x = (low // 2) % 2
    bit_y = low // 4
    first = bit_x * (1 - core) + bit_y * core
    second = bit_y * (1 - core) + bit_x * core
    sibling = me + 1 - 2 * core
    peer_first = me + (1 - 2 * first) * (2 + 2 * core)
    peer_second = me + (1 - 2 * second) * (4 - 2 * core)

    def chain_peer(k):
        return lax.rem(high + k, links) * stride + low

    def remote(src, dst, send, recv, peer):
        return pltpu.make_async_remote_copy(
            src_ref=src,
            dst_ref=dst,
            send_sem=send,
            recv_sem=recv,
            device_id={"seq": peer},
            device_id_type=pl.DeviceIdType.MESH,
        )

    weight_copies = [
        pltpu.make_async_copy(src, dst, weight_sem.at[i])
        for i, (src, dst) in enumerate(
            ((w_in_hbm, w_in), (w_conv_hbm, w_conv), (w_out_hbm, w_out), (w_head_hbm, w_head))
        )
    ]
    for copy in weight_copies:
        copy.start()

    barrier = pltpu.get_barrier_semaphore()
    partners = [sibling, peer_first, peer_second] + [chain_peer(k) for k in range(1, links)]
    for peer in partners:
        pl.semaphore_signal(
            barrier, inc=1, device_id={"seq": peer}, device_id_type=pl.DeviceIdType.MESH
        )
    pl.semaphore_wait(barrier, len(partners))

    own = pl.ds(pl.multiple_of(high * part, part), part)
    regroup = [[], []]
    for which, (src, dst) in enumerate(((features, stream.at[0]), (packed, tracks_in))):
        for k in range(1, links):
            there = pl.ds(pl.multiple_of(lax.rem(high + k, links) * part, part), part)
            copy = remote(
                src.at[there], dst.at[own], a_send.at[which, k], a_recv.at[which, k], chain_peer(k)
            )
            copy.start()
            regroup[which].append(copy)
    stream[0, own, :] = features[own, :]
    tracks_in[own, :] = packed[own, :]

    def swap(value):
        half = value.shape[1] // 2
        return jnp.concatenate([value[:, half:], value[:, :half]], axis=1)

    def mirror(p):
        return rows + (links - 1 - p) * part

    def chunks(count, body):
        def step(i, carry):
            body(pl.ds(pl.multiple_of(i * CHUNK, CHUNK), CHUNK))
            return carry

        lax.fori_loop(0, count // CHUNK, step, 0)

    def chain_chunks(body):
        for p in range(links):

            def step(i, carry, p=p):
                offset = pl.multiple_of(i * CHUNK, CHUNK)
                body(pl.ds(p * part + offset, CHUNK), pl.ds(mirror(p) + offset, CHUNK))
                return carry

            lax.fori_loop(0, part // CHUNK, step, 0)

    def activate(value_ref, slope_ref, layer):
        def body(at):
            v = narrow[at, :]
            square = v * v
            tangent = jnp.tanh(TANH_COEF * (v + CUBIC_COEF * square * v))
            value_ref[layer, at, :] = (0.5 * v * (1.0 + tangent)).astype(BF16)
            slope_ref[layer, at, :] = 0.5 * (1.0 + tangent) + 0.5 * v * (
                1.0 - tangent * tangent
            ) * TANH_COEF * (1.0 + 3.0 * CUBIC_COEF * square)

        chunks(2 * rows, body)

    def strand(s):
        return slice(s * rows, (s + 1) * rows)

    def ends(s, skip):
        return slice(s * rows + skip, (s + 1) * rows), slice(s * rows, (s + 1) * rows - skip)

    steps_of = (1, SECOND_DILATION // FIRST_DILATION)

    for copy in regroup[0]:
        copy.wait()

    def spread(at, across):
        stream[0, across, :] = swap(stream[0, at, :])

    chain_chunks(spread)
    for copy in weight_copies[:3]:
        copy.wait()

    for layer in range(2):
        skip = steps_of[layer] * part
        for s in range(2):
            narrow[strand(s), :] = dot(stream[layer, strand(s), :], w_in[layer])
        activate(hidden, slope_h, layer)
        for s in range(2):
            narrow[strand(s), :] = dot(hidden[layer, strand(s), :], w_conv[layer, 1])
            after, before = ends(s, skip)
            narrow[after, :] += dot(hidden[layer, before, :], w_conv[layer, 0])
            narrow[before, :] += dot(hidden[layer, after, :], w_conv[layer, 2])
        activate(middle, slope_m, layer)
        for s in range(2):
            wide[strand(s), :] = dot(middle[layer, strand(s), :], w_out[layer])

        def add(at, layer=layer):
            stream[layer + 1, at, :] = (stream[layer, at, :].astype(F32) + wide[at, :]).astype(BF16)

        chunks(2 * rows, add)

    def join(at, across):
        joined[at, :] = (
            0.5 * (stream[2, at, :].astype(F32) + swap(stream[2, across, :]).astype(F32))
        ).astype(BF16)

    chain_chunks(join)
    weight_copies[3].wait()
    for copy in regroup[1]:
        copy.wait()
    loss_scale = 1.0 / math.sqrt(rows * n)
    for panel in range(tracks // LANES):
        at_panel = slice(panel * LANES, (panel + 1) * LANES)
        logits = dot(joined[...], w_head[:, at_panel])
        mask = tracks_in[:, tracks:].astype(F32)
        counts = tracks_in[:, at_panel].astype(F32)
        logit_grad[:, at_panel] = (mask * (jnp.exp(logits) - counts) * loss_scale).astype(BF16)
    wide[:rows, :] = dot_t(logit_grad[...], w_head[...])

    def divide(at, across):
        incoming = (0.5 * wide[at, :]).astype(BF16)
        cot[at, :] = incoming
        cot[across, :] = swap(incoming)

    chain_chunks(divide)

    quads = [(h, y, x) for h in range(links) for y in range(2) for x in range(2)]
    per_chip = 2 * hid // n

    def place(layer, half, start, value, height):
        for j, (h, y, x) in enumerate(quads):
            second_i, first_i = (y, x) if half == 0 else (x, y)
            sums[layer, half, h, second_i, first_i, start : start + height, :] = value[
                j * height : (j + 1) * height, :
            ]

    def stage0(layer):
        def step(h, carry):
            for b in range(2):
                for a in range(2):
                    send0[layer, h, b, a] = sums[layer, 1 - core, h, b, a].astype(BF16)
            return carry

        lax.fori_loop(0, links, step, 0)
        copy = remote(
            send0.at[layer], recv0.at[layer], g_send.at[layer, 0], g_recv.at[layer, 0], sibling
        )
        copy.start()
        return [copy]

    def stage1(layer, copies):
        for copy in copies:
            copy.wait()

        def step(h, carry):
            for b in range(2):
                send1[layer, h, b] = (
                    sums[layer, core, h, b, 1 - first]
                    + recv0[layer, h, b, 1 - first].astype(F32)
                ).astype(BF16)
            return carry

        lax.fori_loop(0, links, step, 0)
        copy = remote(
            send1.at[layer], recv1.at[layer], g_send.at[layer, 1], g_recv.at[layer, 1], peer_first
        )
        copy.start()
        return [copy]

    def partial1(layer, h, b):
        return (
            sums[layer, core, h, b, first]
            + recv0[layer, h, b, first].astype(F32)
            + recv1[layer, h, b].astype(F32)
        )

    def stage2(layer, copies):
        for copy in copies:
            copy.wait()

        def step(h, carry):
            send2[layer, h] = partial1(layer, h, 1 - second).astype(BF16)
            return carry

        lax.fori_loop(0, links, step, 0)
        copy = remote(
            send2.at[layer], recv2.at[layer], g_send.at[layer, 2], g_recv.at[layer, 2], peer_second
        )
        copy.start()
        return [copy]

    def partial2(layer, h):
        return partial1(layer, h, second) + recv2[layer, h].astype(F32)

    def stage3(layer, copies):
        for copy in copies:
            copy.wait()
        started = []
        for k in range(1, links):
            send3[layer, k] = partial2(layer, lax.rem(high + k, links)).astype(BF16)
            copy = remote(
                send3.at[layer, k],
                recv3.at[layer, k],
                g_send.at[layer, 3 + k],
                g_recv.at[layer, 3 + k],
                chain_peer(k),
            )
            copy.start()
            started.append(copy)
        return started

    def stage4(layer, copies):
        total = partial2(layer, high)
        for k, copy in enumerate(copies):
            copy.wait()
            total = total + recv3[layer, k + 1].astype(F32)
        final[layer, core] = total
        copy = remote(
            final.at[layer, core],
            final.at[layer, core],
            g_send.at[layer, 3],
            g_recv.at[layer, 3],
            sibling,
        )
        copy.start()
        return [copy]

    pending = None
    for layer in (1, 0):
        skip = steps_of[layer] * part
        grad = grad_dot(middle[layer], cot[...])
        place(layer, 1, per_chip, grad[:, :hid], per_chip)
        place(layer, 1, 2 * per_chip, grad[:, hid:], per_chip)
        for s in range(2):
            narrow[strand(s), :] = dot_t(cot[strand(s), :], w_out[layer])

        def slope(at, layer=layer):
            grad_v[at, :] = (narrow[at, :] * slope_m[layer, at, :]).astype(BF16)

        chunks(2 * rows, slope)
        if pending is not None:
            pending = stage1(1, pending)
        spans = [ends(s, skip) for s in range(2)]

        def joined_rows(read, side):
            return jnp.concatenate([read(spans[s][side]) for s in range(2)], axis=0)

        def read_hidden(at, layer=layer):
            return hidden[layer, at, :]

        def read_grad(at):
            return grad_v[at, :]

        place(
            layer,
            0,
            2 * per_chip,
            grad_dot(joined_rows(read_hidden, 1), joined_rows(read_grad, 0)),
            per_chip,
        )
        place(layer, 0, 3 * per_chip, grad_dot(hidden[layer], grad_v[...]), per_chip)
        place(
            layer,
            1,
            0,
            grad_dot(joined_rows(read_hidden, 0), joined_rows(read_grad, 1)),
            per_chip,
        )
        for s in range(2):
            narrow[strand(s), :] = dot_t(grad_v[strand(s), :], w_conv[layer, 1])
            after, before = ends(s, skip)
            narrow[before, :] += dot_t(grad_v[after, :], w_conv[layer, 0])
            narrow[after, :] += dot_t(grad_v[before, :], w_conv[layer, 2])

        def slope_back(at, layer=layer):
            grad_v[at, :] = (narrow[at, :] * slope_h[layer, at, :]).astype(BF16)

        chunks(2 * rows, slope_back)
        place(layer, 0, 0, grad_dot(stream[layer], grad_v[...]), 2 * per_chip)
        if layer == 1:
            pending = stage0(1)
            for s in range(2):
                wide[strand(s), :] = dot_t(grad_v[strand(s), :], w_in[layer])

            def renew(at):
                cot[at, :] = (cot[at, :].astype(F32) + wide[at, :]).astype(BF16)

            chunks(2 * rows, renew)
    other = stage0(0)
    pending = stage2(1, pending)
    other = stage1(0, other)
    pending = stage3(1, pending)
    other = stage2(0, other)
    pending = stage4(1, pending)
    other = stage3(0, other)
    other = stage4(0, other)
    for copy in pending + other:
        copy.wait()

    dev_rows = per_chip // 2
    for c in range(2):

        @pl.when(core == c)
        def _(c=c):
            for layer in range(2):
                out_in[layer] = final[layer, 0, c * per_chip : (c + 1) * per_chip, :]

                def own_rows(half, start, c=c, layer=layer):
                    block = final[layer, half, start : start + per_chip, :]
                    return block[c * dev_rows : (c + 1) * dev_rows, :]

                out_conv[layer, 0] = own_rows(0, 2 * per_chip)
                out_conv[layer, 1] = own_rows(0, 3 * per_chip)
                out_conv[layer, 2] = own_rows(1, 0)
                out_out[layer, :, :hid] = own_rows(1, per_chip)
                out_out[layer, :, hid:] = own_rows(1, 2 * per_chip)


def local(features, targets, mappable, w_in, w_conv, w_out, w_head):
    rows, channels = features.shape
    n = lax.axis_size("seq")
    links = rows * n // FIRST_DILATION
    hid = w_in.shape[2]
    tracks = targets.shape[1]
    per_chip = 2 * hid // n
    height = 4 * per_chip
    extra = jnp.broadcast_to(mappable[:, None], (rows, LANES))
    packed = jnp.concatenate([targets, extra], axis=1).astype(BF16)
    both = 2 * rows
    vmem = pl.BlockSpec(memory_space=pltpu.VMEM)
    hbm = pl.BlockSpec(memory_space=pl.ANY)
    quad = (links, 2, 2, height, hid)
    return pl.pallas_call(
        functools.partial(kernel, n),
        out_shape=(
            jax.ShapeDtypeStruct((2, channels // n, hid), F32),
            jax.ShapeDtypeStruct((2, 3, hid // n, hid), F32),
            jax.ShapeDtypeStruct((2, hid // n, channels), F32),
        ),
        in_specs=[vmem, vmem, hbm, hbm, hbm, hbm],
        out_specs=(vmem, vmem, vmem),
        scratch_shapes=[
            pltpu.VMEM(w_in.shape, BF16),
            pltpu.VMEM(w_conv.shape, BF16),
            pltpu.VMEM(w_out.shape, BF16),
            pltpu.VMEM(w_head.shape, BF16),
            pltpu.VMEM((3, both, channels), BF16),
            pltpu.VMEM((rows, tracks + LANES), BF16),
            pltpu.VMEM((2, both, hid), BF16),
            pltpu.VMEM((2, both, hid), F32),
            pltpu.VMEM((2, both, hid), BF16),
            pltpu.VMEM((2, both, hid), F32),
            pltpu.VMEM((both, channels), BF16),
            pltpu.VMEM((both, hid), BF16),
            pltpu.VMEM((both, hid), F32),
            pltpu.VMEM((both, channels), F32),
            pltpu.VMEM((rows, channels), BF16),
            pltpu.VMEM((rows, tracks), BF16),
            pltpu.VMEM((2, 2) + quad, F32),
            pltpu.VMEM((2,) + quad, BF16),
            pltpu.VMEM((2,) + quad, BF16),
            pltpu.VMEM((2, links, 2, height, hid), BF16),
            pltpu.VMEM((2, links, 2, height, hid), BF16),
            pltpu.VMEM((2, links, height, hid), BF16),
            pltpu.VMEM((2, links, height, hid), BF16),
            pltpu.VMEM((2, links, height, hid), BF16),
            pltpu.VMEM((2, links, height, hid), BF16),
            pltpu.VMEM((2, 2, height, hid), F32),
            pltpu.SemaphoreType.DMA((4,)),
            pltpu.SemaphoreType.DMA((2, links)),
            pltpu.SemaphoreType.DMA((2, links)),
            pltpu.SemaphoreType.DMA((2, 3 + links)),
            pltpu.SemaphoreType.DMA((2, 3 + links)),
        ],
        compiler_params=pltpu.CompilerParams(
            collective_id=0, has_side_effects=True, vmem_limit_bytes=60 * 1024 * 1024
        ),
    )(features, packed, w_in, w_conv, w_out, w_head)


def solution(mesh):
    in_specs = (
        P(("grp", "seq"), None),
        P(("grp", "seq"), None),
        P(("grp", "seq")),
        P(),
        P(),
        P(),
        P(),
    )
    out_specs = (P("grp", "seq", None), P("grp", None, "seq", None), P("grp", "seq", None))
    return jax.shard_map(local, mesh=mesh, in_specs=in_specs, out_specs=out_specs, check_vma=False)
```

```python
import functools
import math

import jax
import jax.numpy as jnp
from jax import lax
from jax.experimental import pallas as pl
from jax.experimental.pallas import tpu as pltpu
from jax.sharding import PartitionSpec as P

FIRST_DILATION = 2048
SECOND_DILATION = 4096

TANH_COEF = 0.7978845608028654
CUBIC_COEF = 0.044715
LANES = 128
CHUNK = 32
BF16 = jnp.bfloat16
F32 = jnp.float32


def dot(left, right):
    return jnp.dot(left, right, preferred_element_type=F32)


def dot_t(left, right):
    return lax.dot_general(left, right, (((1,), (1,)), ((), ())), preferred_element_type=F32)


def grad_dot(left, right):
    return lax.dot_general(left, right, (((0,), (0,)), ((), ())), preferred_element_type=F32)


def kernel(n, *refs):
    (features, targets, mappable, w_in_hbm, w_conv_hbm, w_out_hbm, w_head_hbm, result) = refs[:8]
    (w_in, w_conv, w_out, w_head, stream, packed, tracks_in) = refs[8:15]
    (hidden, slope_h, middle, slope_m, cot, grad_v, narrow, wide, joined, logit_grad) = refs[15:25]
    chunk_refs = (refs[25:35], refs[35:45])
    (weight_sem, a_send, a_recv, g_send, g_recv) = refs[45:]
    rows, channels = features.shape
    hid = w_in.shape[2]
    tracks = w_head.shape[1]
    links = rows * n // FIRST_DILATION
    part = rows // links
    stride = n // links
    me = lax.axis_index("seq")
    high = me // stride
    low = me % stride
    core = low % 2
    bit_x = (low // 2) % 2
    bit_y = low // 4
    first = bit_x * (1 - core) + bit_y * core
    second = bit_y * (1 - core) + bit_x * core
    sibling = me + 1 - 2 * core
    peer_first = me + (1 - 2 * first) * (2 + 2 * core)
    peer_second = me + (1 - 2 * second) * (4 - 2 * core)

    def chain_peer(k):
        return lax.rem(high + k, links) * stride + low

    def remote(src, dst, send, recv, peer):
        return pltpu.make_async_remote_copy(
            src_ref=src,
            dst_ref=dst,
            send_sem=send,
            recv_sem=recv,
            device_id={"seq": peer},
            device_id_type=pl.DeviceIdType.MESH,
        )

    weight_copies = [
        pltpu.make_async_copy(src, dst, weight_sem.at[i])
        for i, (src, dst) in enumerate(
            ((w_in_hbm, w_in), (w_conv_hbm, w_conv), (w_out_hbm, w_out), (w_head_hbm, w_head))
        )
    ]
    for copy in weight_copies:
        copy.start()

    barrier = pltpu.get_barrier_semaphore()
    partners = [sibling, peer_first, peer_second] + [chain_peer(k) for k in range(1, links)]
    for peer in partners:
        pl.semaphore_signal(
            barrier, inc=1, device_id={"seq": peer}, device_id_type=pl.DeviceIdType.MESH
        )

    def chunks(count, body):
        def step(i, carry):
            body(pl.ds(pl.multiple_of(i * CHUNK, CHUNK), CHUNK))
            return carry

        lax.fori_loop(0, count // CHUNK, step, 0)

    def pack(at):
        packed[at, :tracks] = targets[at, :].astype(F32).astype(BF16)
        packed[at, tracks:] = mappable[at, :].astype(F32).astype(BF16)

    chunks(rows, pack)
    pl.semaphore_wait(barrier, len(partners))

    own = pl.ds(pl.multiple_of(high * part, part), part)
    regroup = [[], []]
    for which, (src, dst) in enumerate(((features, stream.at[0]), (packed, tracks_in))):
        for k in range(1, links):
            there = pl.ds(pl.multiple_of(lax.rem(high + k, links) * part, part), part)
            copy = remote(
                src.at[there], dst.at[own], a_send.at[which, k], a_recv.at[which, k], chain_peer(k)
            )
            copy.start()
            regroup[which].append(copy)
    stream[0, own, :] = features[own, :]
    tracks_in[own, :] = packed[own, :]

    def swap(value):
        half = value.shape[1] // 2
        return jnp.concatenate([value[:, half:], value[:, :half]], axis=1)

    def mirror(p):
        return rows + (links - 1 - p) * part

    def chain_chunks(body):
        for p in range(links):

            def step(i, carry, p=p):
                offset = pl.multiple_of(i * CHUNK, CHUNK)
                body(pl.ds(p * part + offset, CHUNK), pl.ds(mirror(p) + offset, CHUNK))
                return carry

            lax.fori_loop(0, part // CHUNK, step, 0)

    def activate(value_ref, slope_ref, layer):
        def body(at):
            v = narrow[at, :]
            square = v * v
            tangent = jnp.tanh(TANH_COEF * (v + CUBIC_COEF * square * v))
            value_ref[layer, at, :] = (0.5 * v * (1.0 + tangent)).astype(BF16)
            slope_ref[layer, at, :] = 0.5 * (1.0 + tangent) + 0.5 * v * (
                1.0 - tangent * tangent
            ) * TANH_COEF * (1.0 + 3.0 * CUBIC_COEF * square)

        chunks(2 * rows, body)

    def strand(s):
        return slice(s * rows, (s + 1) * rows)

    def ends(s, skip):
        return slice(s * rows + skip, (s + 1) * rows), slice(s * rows, (s + 1) * rows - skip)

    steps_of = (1, SECOND_DILATION // FIRST_DILATION)

    for copy in regroup[0]:
        copy.wait()

    def spread(at, across):
        stream[0, across, :] = swap(stream[0, at, :])

    chain_chunks(spread)
    for copy in weight_copies[:3]:
        copy.wait()

    for layer in range(2):
        skip = steps_of[layer] * part
        for s in range(2):
            narrow[strand(s), :] = dot(stream[layer, strand(s), :], w_in[layer])
        activate(hidden, slope_h, layer)
        for s in range(2):
            narrow[strand(s), :] = dot(hidden[layer, strand(s), :], w_conv[layer, 1])
            after, before = ends(s, skip)
            narrow[after, :] += dot(hidden[layer, before, :], w_conv[layer, 0])
            narrow[before, :] += dot(hidden[layer, after, :], w_conv[layer, 2])
        activate(middle, slope_m, layer)
        for s in range(2):
            wide[strand(s), :] = dot(middle[layer, strand(s), :], w_out[layer])

        def add(at, layer=layer):
            stream[layer + 1, at, :] = (stream[layer, at, :].astype(F32) + wide[at, :]).astype(BF16)

        chunks(2 * rows, add)

    def join(at, across):
        joined[at, :] = (
            0.5 * (stream[2, at, :].astype(F32) + swap(stream[2, across, :]).astype(F32))
        ).astype(BF16)

    chain_chunks(join)
    weight_copies[3].wait()
    for copy in regroup[1]:
        copy.wait()
    loss_scale = 1.0 / math.sqrt(rows * n)
    for panel in range(tracks // LANES):
        at_panel = slice(panel * LANES, (panel + 1) * LANES)
        logits = dot(joined[...], w_head[:, at_panel])
        mask = tracks_in[:, tracks:].astype(F32)
        counts = tracks_in[:, at_panel].astype(F32)
        logit_grad[:, at_panel] = (mask * (jnp.exp(logits) - counts) * loss_scale).astype(BF16)
    wide[:rows, :] = dot_t(logit_grad[...], w_head[...])

    def divide(at, across):
        incoming = (0.5 * wide[at, :]).astype(BF16)
        cot[at, :] = incoming
        cot[across, :] = swap(incoming)

    chain_chunks(divide)

    quads = [(h, y, x) for h in range(links) for y in range(2) for x in range(2)]
    per_chip = 2 * hid // n

    def place(layer, chunk, start, value, height):
        sums = chunk_refs[chunk][0]
        limit = sums.shape[5]
        for half in range(2):
            low_row = max(start, half * limit)
            high_row = min(start + height, (half + 1) * limit)
            if low_row >= high_row:
                continue
            at = slice(low_row - half * limit, high_row - half * limit)
            for j, (h, y, x) in enumerate(quads):
                b, a = (y, x) if half == 0 else (x, y)
                base = j * height - start
                sums[layer, half, h, b, a, at, :] = value[base + low_row : base + high_row, :]

    class Scatter:
        def __init__(self, layer, chunk):
            (self.sums, *pairs, self.final) = chunk_refs[chunk]
            self.send, self.recv = pairs[0::2], pairs[1::2]
            self.layer, self.index = layer, 2 * layer + chunk
            self.stage, self.copies = 0, []

        def start(self, src, dst, sem, peer):
            copy = remote(src, dst, g_send.at[self.index, sem], g_recv.at[self.index, sem], peer)
            copy.start()
            self.copies.append(copy)

        def finish(self):
            for copy in self.copies:
                copy.wait()
            self.copies = []

        def advance(self):
            self.finish()
            getattr(self, "stage%d" % self.stage)()
            self.stage += 1

        def stage0(self):
            def step(h, carry):
                for b in range(2):
                    for a in range(2):
                        self.send[0][self.layer, h, b, a] = self.sums[
                            self.layer, 1 - core, h, b, a
                        ].astype(BF16)
                return carry

            lax.fori_loop(0, links, step, 0)
            self.start(self.send[0].at[self.layer], self.recv[0].at[self.layer], 0, sibling)

        def partial0(self, h, b, a):
            return self.sums[self.layer, core, h, b, a] + self.recv[0][
                self.layer, h, b, a
            ].astype(F32)

        def partial1(self, h, b):
            return self.partial0(h, b, first) + self.recv[1][self.layer, h, b].astype(F32)

        def partial2(self, h):
            return self.partial1(h, second) + self.recv[2][self.layer, h].astype(F32)

        def stage1(self):
            def step(h, carry):
                for b in range(2):
                    self.send[1][self.layer, h, b] = self.partial0(h, b, 1 - first).astype(BF16)
                return carry

            lax.fori_loop(0, links, step, 0)
            self.start(self.send[1].at[self.layer], self.recv[1].at[self.layer], 1, peer_first)

        def stage2(self):
            def step(h, carry):
                self.send[2][self.layer, h] = self.partial1(h, 1 - second).astype(BF16)
                return carry

            lax.fori_loop(0, links, step, 0)
            self.start(self.send[2].at[self.layer], self.recv[2].at[self.layer], 2, peer_second)

        def stage3(self):
            for k in range(1, links):
                self.send[3][self.layer, k] = self.partial2(lax.rem(high + k, links)).astype(BF16)
                self.start(
                    self.send[3].at[self.layer, k],
                    self.recv[3].at[self.layer, k],
                    3 + k,
                    chain_peer(k),
                )

        def stage4(self):
            total = self.partial2(high)
            for k in range(1, links):
                total = total + self.recv[3][self.layer, k].astype(F32)
            self.final[self.layer, core] = total
            here = self.final.at[self.layer, core]
            self.start(here, here, 3, sibling)

    wide_1, tall_1, wide_0, tall_0 = [Scatter(layer, chunk) for layer in (1, 0) for chunk in (0, 1)]

    for layer in (1, 0):
        skip = steps_of[layer] * part
        grad = grad_dot(middle[layer], cot[...])
        place(layer, 0, 3 * per_chip, grad[:, :hid], per_chip)
        place(layer, 0, 4 * per_chip, grad[:, hid:], per_chip)
        for s in range(2):
            narrow[strand(s), :] = dot_t(cot[strand(s), :], w_out[layer])

        def slope(at, layer=layer):
            grad_v[at, :] = (narrow[at, :] * slope_m[layer, at, :]).astype(BF16)

        chunks(2 * rows, slope)
        if layer == 0:
            tall_1.advance()
        spans = [ends(s, skip) for s in range(2)]

        def joined_rows(read, side):
            return jnp.concatenate([read(spans[s][side]) for s in range(2)], axis=0)

        def read_hidden(at, layer=layer):
            return hidden[layer, at, :]

        def read_grad(at):
            return grad_v[at, :]

        place(
            layer,
            0,
            0,
            grad_dot(joined_rows(read_hidden, 1), joined_rows(read_grad, 0)),
            per_chip,
        )
        place(layer, 0, per_chip, grad_dot(hidden[layer], grad_v[...]), per_chip)
        place(
            layer,
            0,
            2 * per_chip,
            grad_dot(joined_rows(read_hidden, 0), joined_rows(read_grad, 1)),
            per_chip,
        )
        if layer == 0:
            wide_1.advance()
        (wide_0, wide_1)[layer].advance()
        for s in range(2):
            narrow[strand(s), :] = dot_t(grad_v[strand(s), :], w_conv[layer, 1])
            after, before = ends(s, skip)
            narrow[before, :] += dot_t(grad_v[after, :], w_conv[layer, 0])
            narrow[after, :] += dot_t(grad_v[before, :], w_conv[layer, 2])

        def slope_back(at, layer=layer):
            grad_v[at, :] = (narrow[at, :] * slope_h[layer, at, :]).astype(BF16)

        chunks(2 * rows, slope_back)
        if layer == 0:
            wide_1.advance()
            tall_1.advance()
        (wide_0, wide_1)[layer].advance()
        place(layer, 1, 0, grad_dot(stream[layer], grad_v[...]), 2 * per_chip)
        if layer == 1:
            tall_1.advance()
            for s in range(2):
                wide[strand(s), :] = dot_t(grad_v[strand(s), :], w_in[layer])

            def renew(at):
                cot[at, :] = (cot[at, :].astype(F32) + wide[at, :]).astype(BF16)

            chunks(2 * rows, renew)
    tall_0.advance()
    for scatter in (wide_1, tall_1, wide_0, tall_0, tall_1, wide_0, tall_0, wide_0, tall_0, tall_0):
        scatter.advance()
    for scatter in (wide_1, tall_1, wide_0, tall_0):
        assert scatter.stage == 5
        scatter.finish()
    (wide_final, tall_final) = (chunk_refs[0][-1], chunk_refs[1][-1])
    limit = wide_final.shape[2]
    result[:, :, :limit, :] = wide_final[...]
    result[:, :, limit:, :] = tall_final[...]


def deliver(limit, per_chip, result, out_in, out_conv, out_out):
    core = lax.axis_index("seq") % 2
    hid = result.shape[3]
    own = per_chip // 2
    height = result.shape[2] - limit

    def rows_of(layer, base, size, start, count):
        pieces = []
        for half in range(2):
            low_row = max(start, half * size)
            high_row = min(start + count, (half + 1) * size)
            if low_row < high_row:
                offset = base - half * size
                pieces.append(result[layer, half, offset + low_row : offset + high_row, :])
        return pieces[0] if len(pieces) == 1 else jnp.concatenate(pieces, axis=0)

    for c in range(2):

        @pl.when(core == c)
        def _(c=c):
            for layer in range(2):
                out_in[layer] = rows_of(layer, limit, height, c * per_chip, per_chip)
                for t in range(3):
                    out_conv[t, :, layer, :] = rows_of(layer, 0, limit, t * per_chip + c * own, own)
                for t in range(2):
                    out_out[:, layer, t * hid : (t + 1) * hid] = rows_of(
                        layer, 0, limit, (3 + t) * per_chip + c * own, own
                    )


def local(features, targets, mappable, w_in, w_conv, w_out, w_head):
    rows, channels = features.shape
    n = lax.axis_size("seq")
    links = rows * n // FIRST_DILATION
    hid = w_in.shape[2]
    tracks = targets.shape[1]
    per_chip = 2 * hid // n
    heights = [(5 * per_chip + 31) // 32 * 16, (2 * per_chip + 31) // 32 * 16]
    mappable = jnp.broadcast_to(mappable[:, None], (rows, LANES))
    both = 2 * rows
    vmem = pl.BlockSpec(memory_space=pltpu.VMEM)
    hbm = pl.BlockSpec(memory_space=pl.ANY)
    chunk_shapes = []
    for height in heights:
        quad = (links, 2, 2, height, hid)
        chunk_shapes += [
            pltpu.VMEM((2, 2) + quad, F32),
            pltpu.VMEM((2,) + quad, BF16),
            pltpu.VMEM((2,) + quad, BF16),
            pltpu.VMEM((2, links, 2, height, hid), BF16),
            pltpu.VMEM((2, links, 2, height, hid), BF16),
            pltpu.VMEM((2, links, height, hid), BF16),
            pltpu.VMEM((2, links, height, hid), BF16),
            pltpu.VMEM((2, links, height, hid), BF16),
            pltpu.VMEM((2, links, height, hid), BF16),
            pltpu.VMEM((2, 2, height, hid), F32),
        ]
    result = pl.pallas_call(
        functools.partial(kernel, n),
        out_shape=jax.ShapeDtypeStruct((2, 2, sum(heights), hid), F32),
        in_specs=[vmem, vmem, vmem, hbm, hbm, hbm, hbm],
        out_specs=vmem,
        scratch_shapes=[
            pltpu.VMEM(w_in.shape, BF16),
            pltpu.VMEM(w_conv.shape, BF16),
            pltpu.VMEM(w_out.shape, BF16),
            pltpu.VMEM(w_head.shape, BF16),
            pltpu.VMEM((3, both, channels), BF16),
            pltpu.VMEM((rows, tracks + LANES), BF16),
            pltpu.VMEM((rows, tracks + LANES), BF16),
            pltpu.VMEM((2, both, hid), BF16),
            pltpu.VMEM((2, both, hid), F32),
            pltpu.VMEM((2, both, hid), BF16),
            pltpu.VMEM((2, both, hid), F32),
            pltpu.VMEM((both, channels), BF16),
            pltpu.VMEM((both, hid), BF16),
            pltpu.VMEM((both, hid), F32),
            pltpu.VMEM((both, channels), F32),
            pltpu.VMEM((rows, channels), BF16),
            pltpu.VMEM((rows, tracks), BF16),
            *chunk_shapes,
            pltpu.SemaphoreType.DMA((4,)),
            pltpu.SemaphoreType.DMA((2, links)),
            pltpu.SemaphoreType.DMA((2, links)),
            pltpu.SemaphoreType.DMA((4, 3 + links)),
            pltpu.SemaphoreType.DMA((4, 3 + links)),
        ],
        compiler_params=pltpu.CompilerParams(
            collective_id=0, has_side_effects=True, vmem_limit_bytes=60 * 1024 * 1024
        ),
    )(features, targets, mappable, w_in, w_conv, w_out, w_head)
    grad_in, grad_conv, grad_out = pl.pallas_call(
        functools.partial(deliver, heights[0], per_chip),
        out_shape=(
            jax.ShapeDtypeStruct((2, channels // n, hid), F32),
            jax.ShapeDtypeStruct((3, hid // n, 2, hid), F32),
            jax.ShapeDtypeStruct((hid // n, 2, channels), F32),
        ),
        in_specs=[vmem],
        out_specs=(vmem, vmem, vmem),
    )(result)
    return (grad_in, jnp.transpose(grad_conv, (2, 0, 1, 3)), jnp.transpose(grad_out, (1, 0, 2)))


def solution(mesh):
    in_specs = (
        P(("grp", "seq"), None),
        P(("grp", "seq"), None),
        P(("grp", "seq")),
        P(),
        P(),
        P(),
        P(),
    )
    out_specs = (P("grp", "seq", None), P("grp", None, "seq", None), P("grp", "seq", None))
    return jax.shard_map(local, mesh=mesh, in_specs=in_specs, out_specs=out_specs, check_vma=False)
```

```python
import functools
import math

import jax
import jax.numpy as jnp
from jax import lax
from jax.experimental import pallas as pl
from jax.experimental.pallas import tpu as pltpu
from jax.sharding import PartitionSpec as P

FIRST_DILATION = 2048
SECOND_DILATION = 4096

TANH_COEF = 0.7978845608028654
CUBIC_COEF = 0.044715
LANES = 128
CHUNK = 32
BF16 = jnp.bfloat16
F32 = jnp.float32


def dot(left, right):
    return jnp.dot(left, right, preferred_element_type=F32)


def dot_t(left, right):
    return lax.dot_general(left, right, (((1,), (1,)), ((), ())), preferred_element_type=F32)


def grad_dot(left, right):
    return lax.dot_general(left, right, (((0,), (0,)), ((), ())), preferred_element_type=F32)


def kernel(n, *refs):
    (features, targets, mappable, w_in_hbm, w_conv_hbm, w_out_hbm, w_head_hbm, result) = refs[:8]
    (w_in, w_conv, w_out, w_head, stream, packed, tracks_in) = refs[8:15]
    (hidden, slope_h, middle, slope_m, cot, grad_v, narrow, wide, joined, logit_grad) = refs[15:25]
    chunk_refs = (refs[25:35], refs[35:45])
    (weight_sem, a_send, a_recv, g_send, g_recv) = refs[45:]
    rows, channels = features.shape
    hid = w_in.shape[2]
    tracks = w_head.shape[1]
    links = rows * n // FIRST_DILATION
    part = rows // links
    stride = n // links
    me = lax.axis_index("seq")
    high = me // stride
    low = me % stride
    core = low % 2
    bit_x = (low // 2) % 2
    bit_y = low // 4
    first = bit_x * (1 - core) + bit_y * core
    second = bit_y * (1 - core) + bit_x * core
    sibling = me + 1 - 2 * core
    peer_first = me + (1 - 2 * first) * (2 + 2 * core)
    peer_second = me + (1 - 2 * second) * (4 - 2 * core)

    def chain_peer(k):
        return lax.rem(high + k, links) * stride + low

    def remote(src, dst, send, recv, peer):
        return pltpu.make_async_remote_copy(
            src_ref=src,
            dst_ref=dst,
            send_sem=send,
            recv_sem=recv,
            device_id={"seq": peer},
            device_id_type=pl.DeviceIdType.MESH,
        )

    weight_copies = [
        pltpu.make_async_copy(src, dst, weight_sem.at[i])
        for i, (src, dst) in enumerate(
            ((w_in_hbm, w_in), (w_conv_hbm, w_conv), (w_out_hbm, w_out), (w_head_hbm, w_head))
        )
    ]
    for copy in weight_copies:
        copy.start()

    barrier = pltpu.get_barrier_semaphore()
    partners = [sibling, peer_first, peer_second] + [chain_peer(k) for k in range(1, links)]
    for peer in partners:
        pl.semaphore_signal(
            barrier, inc=1, device_id={"seq": peer}, device_id_type=pl.DeviceIdType.MESH
        )

    def chunks(count, body):
        def step(i, carry):
            body(pl.ds(pl.multiple_of(i * CHUNK, CHUNK), CHUNK))
            return carry

        lax.fori_loop(0, count // CHUNK, step, 0)

    def pack(at):
        packed[at, :tracks] = targets[at, :].astype(F32).astype(BF16)
        packed[at, tracks:] = mappable[at, :].astype(F32).astype(BF16)

    chunks(rows, pack)
    pl.semaphore_wait(barrier, len(partners))

    own = pl.ds(pl.multiple_of(high * part, part), part)
    regroup = [[], []]
    for which, (src, dst) in enumerate(((features, stream.at[0]), (packed, tracks_in))):
        for k in range(1, links):
            there = pl.ds(pl.multiple_of(lax.rem(high + k, links) * part, part), part)
            copy = remote(
                src.at[there], dst.at[own], a_send.at[which, k], a_recv.at[which, k], chain_peer(k)
            )
            copy.start()
            regroup[which].append(copy)
    stream[0, own, :] = features[own, :]
    tracks_in[own, :] = packed[own, :]

    def swap(value):
        half = value.shape[1] // 2
        return jnp.concatenate([value[:, half:], value[:, :half]], axis=1)

    def mirror(p):
        return rows + (links - 1 - p) * part

    def chain_chunks(body):
        for p in range(links):

            def step(i, carry, p=p):
                offset = pl.multiple_of(i * CHUNK, CHUNK)
                body(pl.ds(p * part + offset, CHUNK), pl.ds(mirror(p) + offset, CHUNK))
                return carry

            lax.fori_loop(0, part // CHUNK, step, 0)

    def activate(value_ref, slope_ref, layer):
        def body(at):
            v = narrow[at, :]
            square = v * v
            tangent = jnp.tanh(TANH_COEF * (v + CUBIC_COEF * square * v))
            value_ref[layer, at, :] = (0.5 * v * (1.0 + tangent)).astype(BF16)
            slope_ref[layer, at, :] = 0.5 * (1.0 + tangent) + 0.5 * v * (
                1.0 - tangent * tangent
            ) * TANH_COEF * (1.0 + 3.0 * CUBIC_COEF * square)

        chunks(2 * rows, body)

    def strand(s):
        return slice(s * rows, (s + 1) * rows)

    def ends(s, skip):
        return slice(s * rows + skip, (s + 1) * rows), slice(s * rows, (s + 1) * rows - skip)

    steps_of = (1, SECOND_DILATION // FIRST_DILATION)

    for copy in regroup[0]:
        copy.wait()

    def spread(at, across):
        stream[0, across, :] = swap(stream[0, at, :])

    chain_chunks(spread)
    for copy in weight_copies[:3]:
        copy.wait()

    for layer in range(2):
        skip = steps_of[layer] * part
        for s in range(2):
            narrow[strand(s), :] = dot(stream[layer, strand(s), :], w_in[layer])
        activate(hidden, slope_h, layer)
        for s in range(2):
            narrow[strand(s), :] = dot(hidden[layer, strand(s), :], w_conv[layer, 1])
            after, before = ends(s, skip)
            narrow[after, :] += dot(hidden[layer, before, :], w_conv[layer, 0])
            narrow[before, :] += dot(hidden[layer, after, :], w_conv[layer, 2])
        activate(middle, slope_m, layer)
        for s in range(2):
            wide[strand(s), :] = dot(middle[layer, strand(s), :], w_out[layer])

        def add(at, layer=layer):
            stream[layer + 1, at, :] = (stream[layer, at, :].astype(F32) + wide[at, :]).astype(BF16)

        chunks(2 * rows, add)

    def join(at, across):
        joined[at, :] = (
            0.5 * (stream[2, at, :].astype(F32) + swap(stream[2, across, :]).astype(F32))
        ).astype(BF16)

    chain_chunks(join)
    weight_copies[3].wait()
    for copy in regroup[1]:
        copy.wait()
    loss_scale = 1.0 / math.sqrt(rows * n)
    for panel in range(tracks // LANES):
        at_panel = slice(panel * LANES, (panel + 1) * LANES)
        logits = dot(joined[...], w_head[:, at_panel])
        mask = tracks_in[:, tracks:].astype(F32)
        counts = tracks_in[:, at_panel].astype(F32)
        logit_grad[:, at_panel] = (mask * (jnp.exp(logits) - counts) * loss_scale).astype(BF16)
    wide[:rows, :] = dot_t(logit_grad[...], w_head[...])

    def divide(at, across):
        incoming = (0.5 * wide[at, :]).astype(BF16)
        cot[at, :] = incoming
        cot[across, :] = swap(incoming)

    chain_chunks(divide)

    quads = [(h, y, x) for h in range(links) for y in range(2) for x in range(2)]
    per_chip = 2 * hid // n

    def place(layer, chunk, start, value, height):
        sums = chunk_refs[chunk][0]
        limit = sums.shape[5]
        for half in range(2):
            low_row = max(start, half * limit)
            high_row = min(start + height, (half + 1) * limit)
            if low_row >= high_row:
                continue
            at = slice(low_row - half * limit, high_row - half * limit)
            for j, (h, y, x) in enumerate(quads):
                b, a = (y, x) if half == 0 else (x, y)
                base = j * height - start
                sums[layer, half, h, b, a, at, :] = value[base + low_row : base + high_row, :]

    class Scatter:
        def __init__(self, layer, chunk):
            (self.sums, *pairs, self.final) = chunk_refs[chunk]
            self.send, self.recv = pairs[0::2], pairs[1::2]
            self.layer, self.index = layer, 2 * layer + chunk
            self.stage, self.copies = 0, []

        def start(self, src, dst, sem, peer):
            copy = remote(src, dst, g_send.at[self.index, sem], g_recv.at[self.index, sem], peer)
            copy.start()
            self.copies.append(copy)

        def finish(self):
            for copy in self.copies:
                copy.wait()
            self.copies = []

        def advance(self):
            self.finish()
            getattr(self, "stage%d" % self.stage)()
            self.stage += 1

        def stage0(self):
            def step(h, carry):
                for b in range(2):
                    for a in range(2):
                        self.send[0][self.layer, h, b, a] = self.sums[
                            self.layer, 1 - core, h, b, a
                        ].astype(BF16)
                return carry

            lax.fori_loop(0, links, step, 0)
            self.start(self.send[0].at[self.layer], self.recv[0].at[self.layer], 0, sibling)

        def partial0(self, h, b, a):
            return self.sums[self.layer, core, h, b, a] + self.recv[0][
                self.layer, h, b, a
            ].astype(F32)

        def partial1(self, h, b):
            return self.partial0(h, b, first) + self.recv[1][self.layer, h, b].astype(F32)

        def partial2(self, h):
            return self.partial1(h, second) + self.recv[2][self.layer, h].astype(F32)

        def stage1(self):
            def step(h, carry):
                for b in range(2):
                    self.send[1][self.layer, h, b] = self.partial0(h, b, 1 - first).astype(BF16)
                return carry

            lax.fori_loop(0, links, step, 0)
            self.start(self.send[1].at[self.layer], self.recv[1].at[self.layer], 1, peer_first)

        def stage2(self):
            def step(h, carry):
                self.send[2][self.layer, h] = self.partial1(h, 1 - second).astype(BF16)
                return carry

            lax.fori_loop(0, links, step, 0)
            self.start(self.send[2].at[self.layer], self.recv[2].at[self.layer], 2, peer_second)

        def stage3(self):
            for k in range(1, links):
                self.send[3][self.layer, k] = self.partial2(lax.rem(high + k, links)).astype(BF16)
                self.start(
                    self.send[3].at[self.layer, k],
                    self.recv[3].at[self.layer, k],
                    3 + k,
                    chain_peer(k),
                )

        def stage4(self):
            total = self.partial2(high)
            for k in range(1, links):
                total = total + self.recv[3][self.layer, k].astype(F32)
            self.final[self.layer, core] = total
            here = self.final.at[self.layer, core]
            self.start(here, here, 3, sibling)

    wide_1, tall_1, wide_0, tall_0 = [Scatter(layer, chunk) for layer in (1, 0) for chunk in (0, 1)]

    for layer in (1, 0):
        skip = steps_of[layer] * part
        grad = grad_dot(middle[layer], cot[...])
        place(layer, 0, 3 * per_chip, grad[:, :hid], per_chip)
        place(layer, 0, 4 * per_chip, grad[:, hid:], per_chip)
        for s in range(2):
            narrow[strand(s), :] = dot_t(cot[strand(s), :], w_out[layer])

        def slope(at, layer=layer):
            grad_v[at, :] = (narrow[at, :] * slope_m[layer, at, :]).astype(BF16)

        chunks(2 * rows, slope)
        if layer == 0:
            tall_1.advance()
        spans = [ends(s, skip) for s in range(2)]

        def joined_rows(read, side):
            return jnp.concatenate([read(spans[s][side]) for s in range(2)], axis=0)

        def read_hidden(at, layer=layer):
            return hidden[layer, at, :]

        def read_grad(at):
            return grad_v[at, :]

        place(
            layer,
            0,
            0,
            grad_dot(joined_rows(read_hidden, 1), joined_rows(read_grad, 0)),
            per_chip,
        )
        place(layer, 0, per_chip, grad_dot(hidden[layer], grad_v[...]), per_chip)
        place(
            layer,
            0,
            2 * per_chip,
            grad_dot(joined_rows(read_hidden, 0), joined_rows(read_grad, 1)),
            per_chip,
        )
        if layer == 0:
            wide_1.advance()
        (wide_0, wide_1)[layer].advance()
        for s in range(2):
            narrow[strand(s), :] = dot_t(grad_v[strand(s), :], w_conv[layer, 1])
            after, before = ends(s, skip)
            narrow[before, :] += dot_t(grad_v[after, :], w_conv[layer, 0])
            narrow[after, :] += dot_t(grad_v[before, :], w_conv[layer, 2])

        def slope_back(at, layer=layer):
            grad_v[at, :] = (narrow[at, :] * slope_h[layer, at, :]).astype(BF16)

        chunks(2 * rows, slope_back)
        if layer == 0:
            wide_1.advance()
            tall_1.advance()
        (wide_0, wide_1)[layer].advance()
        place(layer, 1, 0, grad_dot(stream[layer], grad_v[...]), 2 * per_chip)
        if layer == 1:
            tall_1.advance()
            for s in range(2):
                wide[strand(s), :] = dot_t(grad_v[strand(s), :], w_in[layer])

            def renew(at):
                cot[at, :] = (cot[at, :].astype(F32) + wide[at, :]).astype(BF16)

            chunks(2 * rows, renew)
    tall_0.advance()
    for scatter in (tall_0, wide_1, tall_1, wide_0, tall_1, wide_0, tall_0, wide_0, tall_0, tall_0):
        scatter.advance()
    for scatter in (wide_1, tall_1, wide_0, tall_0):
        assert scatter.stage == 5
        scatter.finish()
    (wide_final, tall_final) = (chunk_refs[0][-1], chunk_refs[1][-1])
    limit = wide_final.shape[2]
    result[:, :, :limit, :] = wide_final[...]
    result[:, :, limit:, :] = tall_final[...]


def deliver(limit, per_chip, result, out_in, out_conv, out_out):
    core = lax.axis_index("seq") % 2
    hid = result.shape[3]
    own = per_chip // 2
    height = result.shape[2] - limit

    def rows_of(layer, base, size, start, count):
        pieces = []
        for half in range(2):
            low_row = max(start, half * size)
            high_row = min(start + count, (half + 1) * size)
            if low_row < high_row:
                offset = base - half * size
                pieces.append(result[layer, half, offset + low_row : offset + high_row, :])
        return pieces[0] if len(pieces) == 1 else jnp.concatenate(pieces, axis=0)

    for c in range(2):

        @pl.when(core == c)
        def _(c=c):
            for layer in range(2):
                out_in[layer] = rows_of(layer, limit, height, c * per_chip, per_chip)
                for t in range(3):
                    out_conv[t, :, layer, :] = rows_of(layer, 0, limit, t * per_chip + c * own, own)
                for t in range(2):
                    out_out[:, layer, t * hid : (t + 1) * hid] = rows_of(
                        layer, 0, limit, (3 + t) * per_chip + c * own, own
                    )


def local(features, targets, mappable, w_in, w_conv, w_out, w_head):
    rows, channels = features.shape
    n = lax.axis_size("seq")
    links = rows * n // FIRST_DILATION
    hid = w_in.shape[2]
    tracks = targets.shape[1]
    per_chip = 2 * hid // n
    heights = [(5 * per_chip + 31) // 32 * 16, (2 * per_chip + 31) // 32 * 16]
    mappable = jnp.broadcast_to(mappable[:, None], (rows, LANES))
    both = 2 * rows
    vmem = pl.BlockSpec(memory_space=pltpu.VMEM)
    hbm = pl.BlockSpec(memory_space=pl.ANY)
    chunk_shapes = []
    for height in heights:
        quad = (links, 2, 2, height, hid)
        chunk_shapes += [
            pltpu.VMEM((2, 2) + quad, F32),
            pltpu.VMEM((2,) + quad, BF16),
            pltpu.VMEM((2,) + quad, BF16),
            pltpu.VMEM((2, links, 2, height, hid), BF16),
            pltpu.VMEM((2, links, 2, height, hid), BF16),
            pltpu.VMEM((2, links, height, hid), BF16),
            pltpu.VMEM((2, links, height, hid), BF16),
            pltpu.VMEM((2, links, height, hid), BF16),
            pltpu.VMEM((2, links, height, hid), BF16),
            pltpu.VMEM((2, 2, height, hid), F32),
        ]
    result = pl.pallas_call(
        functools.partial(kernel, n),
        out_shape=jax.ShapeDtypeStruct((2, 2, sum(heights), hid), F32),
        in_specs=[vmem, vmem, vmem, hbm, hbm, hbm, hbm],
        out_specs=vmem,
        scratch_shapes=[
            pltpu.VMEM(w_in.shape, BF16),
            pltpu.VMEM(w_conv.shape, BF16),
            pltpu.VMEM(w_out.shape, BF16),
            pltpu.VMEM(w_head.shape, BF16),
            pltpu.VMEM((3, both, channels), BF16),
            pltpu.VMEM((rows, tracks + LANES), BF16),
            pltpu.VMEM((rows, tracks + LANES), BF16),
            pltpu.VMEM((2, both, hid), BF16),
            pltpu.VMEM((2, both, hid), F32),
            pltpu.VMEM((2, both, hid), BF16),
            pltpu.VMEM((2, both, hid), F32),
            pltpu.VMEM((both, channels), BF16),
            pltpu.VMEM((both, hid), BF16),
            pltpu.VMEM((both, hid), F32),
            pltpu.VMEM((both, channels), F32),
            pltpu.VMEM((rows, channels), BF16),
            pltpu.VMEM((rows, tracks), BF16),
            *chunk_shapes,
            pltpu.SemaphoreType.DMA((4,)),
            pltpu.SemaphoreType.DMA((2, links)),
            pltpu.SemaphoreType.DMA((2, links)),
            pltpu.SemaphoreType.DMA((4, 3 + links)),
            pltpu.SemaphoreType.DMA((4, 3 + links)),
        ],
        compiler_params=pltpu.CompilerParams(
            collective_id=0, has_side_effects=True, vmem_limit_bytes=60 * 1024 * 1024
        ),
    )(features, targets, mappable, w_in, w_conv, w_out, w_head)
    grad_in, grad_conv, grad_out = pl.pallas_call(
        functools.partial(deliver, heights[0], per_chip),
        out_shape=(
            jax.ShapeDtypeStruct((2, channels // n, hid), F32),
            jax.ShapeDtypeStruct((3, hid // n, 2, hid), F32),
            jax.ShapeDtypeStruct((hid // n, 2, channels), F32),
        ),
        in_specs=[vmem],
        out_specs=(vmem, vmem, vmem),
    )(result)
    return (grad_in, jnp.transpose(grad_conv, (2, 0, 1, 3)), jnp.transpose(grad_out, (1, 0, 2)))


def solution(mesh):
    in_specs = (
        P(("grp", "seq"), None),
        P(("grp", "seq"), None),
        P(("grp", "seq")),
        P(),
        P(),
        P(),
        P(),
    )
    out_specs = (P("grp", "seq", None), P("grp", None, "seq", None), P("grp", "seq", None))
    return jax.shard_map(local, mesh=mesh, in_specs=in_specs, out_specs=out_specs, check_vma=False)
```
